128 devices in a mesh: section: 16 (over z, x), bond: 8 (over y, core).
Axes of the slice: x: 4, y: 4, z: 4, core: 2. Of those that a mesh axis runs over, the one named last changes fastest.
Arguments:
- site_tensor: float32 [16, 3072, 4, 3072], P('section', None, None, 'bond'), may hold values from -0.109375 to 0.109375
- boundary: float32 [128, 3072], replicated, may hold values from -6 to 6
- selected: int32 [16, 128], P('section'), may hold values from 0 to 3
Outputs:
- chosen_prob: float32 [16, 128], P('section')
- exit_rows: float32 [16, 128, 3072], P('section', None, 'bond')
The draws below stay inside these ranges and needn't reach their ends.
All inputs are finite; a program needn't handle non-finite values.
Results may differ from the reference program's by a relative error of at most 0.0003.
Values sent between devices are 32-bit elements; how exact they have to be, the bound alone decides.
A program may use at most 128 MiB of HBM per device.

```python
import jax
import jax.numpy as jnp
from jax import lax

CHI = 3072
D = 4
ROWS = 128
SITES = 16


def with_ends(result, own_key, smallest, largest):
    extent = result.shape
    place = [jax.random.randint(jax.random.fold_in(own_key, axis), (), 0, extent[axis]) for axis in range(len(extent))]
    result = result.at[tuple(place)].set(smallest)
    longest = extent.index(max(extent))
    place[longest] = (place[longest] + 1) % extent[longest]
    return result.at[tuple(place)].set(largest)


def steps_of(rng, extent, pieces, smallest, largest):
    level, own = 1.0, jax.random.fold_in(rng, 6)
    for dim, parts in pieces:
        heights = jnp.exp(jax.random.uniform(jax.random.fold_in(own, dim), (parts,), jnp.float32, smallest / len(pieces), largest / len(pieces)))
        level = level * jnp.repeat(heights, extent[dim] // parts).reshape([-1 if axis == dim else 1 for axis in range(len(extent))])
    return level


def noise(stream_key, shape, deviation, limit, shards=(), kind=jnp.bfloat16):
    loudness = steps_of(stream_key, shape, shards, -0.22, 0.18) if shards else 1.0
    array = jax.random.normal(stream_key, shape, jnp.float32) * deviation * loudness
    return jnp.minimum(jnp.maximum(array, -limit), limit).astype(kind)


def setup_inputs(seed: int = 0) -> dict:
    arg_keys = jax.random.split(jax.random.key(seed), 4)
    return {
        "site_tensor": noise(arg_keys[0], (SITES, CHI, D, CHI), CHI ** -0.5, 0.109375, ((0, 16), (3, 8)), jnp.float32),
        "boundary": noise(arg_keys[1], (ROWS, CHI), 1.0, 6.0, (), jnp.float32),
        "selected": with_ends(jax.random.randint(arg_keys[2], (SITES, ROWS), 0, D), jax.random.fold_in(arg_keys[2], 1), 0, D - 1).astype(jnp.int32),
    }


def reference(site_tensor, boundary, selected):
    outcome_ids = jnp.arange(D, dtype=jnp.int32)

    def one_site(left_row, inputs):
        tensor, picks = inputs
        amplitudes = jnp.einsum('ri,ikj->rkj', left_row, tensor, precision=lax.Precision.HIGHEST)
        weight = lax.optimization_barrier(jnp.sum(amplitudes * amplitudes, axis=2))
        onehot = (picks[:, None] == outcome_ids[None, :]).astype(jnp.float32)
        chosen_weight = lax.optimization_barrier(jnp.sum(onehot * weight, axis=1))
        prob = chosen_weight / lax.optimization_barrier(jnp.sum(weight, axis=1))
        chosen_row = lax.optimization_barrier(jnp.sum(onehot[:, :, None] * amplitudes, axis=1))
        next_row = chosen_row / jnp.sqrt(chosen_weight / CHI + 1e-06)[:, None]
        return (next_row, (prob, next_row))
    final_row, outputs = lax.scan(one_site, boundary, (site_tensor, selected))
    return (outputs[0], outputs[1])
```

```python
import functools

import jax
import jax.numpy as jnp
from jax import lax
from jax.experimental import pallas as pl
from jax.experimental.pallas import tpu as pltpu
from jax.sharding import PartitionSpec as P

MESH = pl.DeviceIdType.MESH
BATCH = 8
FILL = 192
SLOTS = 4
DIRECT = ((1, 0), (1, 1), (2, 0), (2, 1), (3, 0), (3, 1), (0, 0), (0, 1))
ORDER = (3, 0, 1, 2)


def kernel(
    sel_ref, w_hbm, start_hbm, prob_ref, rows_ref,
    stage, whi, wlo, left, chosen_rows, acc, picks, part, totals, inverse,
    fill_sem, start_sem, send_sem, recv_sem, wsend_sem, wrecv_sem,
):
    rows, width = left.shape
    outcomes, columns = w_hbm.shape[2], w_hbm.shape[3]
    sections, peers = lax.axis_size("section"), lax.axis_size("bond")
    chips = peers // 2
    batches = rows // BATCH
    fills = width // FILL
    section, me = lax.axis_index("section"), lax.axis_index("bond")
    y, core = me // 2, lax.rem(me, 2)
    following = lax.rem(section + 1, sections)
    before = lax.rem(section + sections - 1, sections)
    first, last = section == 0, section == sections - 1

    def fill(step):
        slot = lax.rem(step, SLOTS)
        return pltpu.make_async_copy(
            w_hbm.at[0, pl.ds(step * FILL, FILL)], stage.at[slot], fill_sem.at[slot]
        )

    for step in range(SLOTS):
        fill(step).start()

    @pl.when(first)
    def _():
        pltpu.make_async_copy(start_hbm, left, start_sem).start()

    barrier = pltpu.get_barrier_semaphore()
    for peer in range(peers):
        for other in (before, following):
            pl.semaphore_signal(barrier, inc=1, device_id=(other, peer), device_id_type=MESH)
    for ahead in range(1, peers):
        pl.semaphore_signal(
            barrier, inc=1, device_id=(section, lax.rem(me + ahead, peers)), device_id_type=MESH
        )

    picks[...] = jnp.broadcast_to(sel_ref[...].astype(jnp.float32), (rows, rows)).T

    def split(step, _):
        slot = lax.rem(step, SLOTS)
        fill(step).wait()

        def some(piece, _):
            row = pl.multiple_of(piece * 32, 32)
            for k in range(outcomes):
                whole = stage[slot, pl.ds(row, 32), k, :]
                high = whole.astype(jnp.bfloat16)
                low = (whole - high.astype(jnp.float32)).astype(jnp.bfloat16)
                at = pl.ds(pl.multiple_of(step * FILL + row, 32), 32)
                whi[at, k * columns : (k + 1) * columns] = high
                wlo[at, k * columns : (k + 1) * columns] = low
            return 0

        lax.fori_loop(0, FILL // 32, some, 0)

        @pl.when(step + SLOTS < fills)
        def _():
            fill(step + SLOTS).start()

        return 0

    lax.fori_loop(0, fills, split, 0)

    pl.semaphore_wait(barrier, 3 * peers - 1)

    @pl.when(first)
    def _():
        pltpu.make_async_copy(start_hbm, left, start_sem).wait()

    def send(batch, index):
        ahead, other = DIRECT[index]
        peer = lax.rem(y + ahead, chips) * 2 + (lax.rem(core + 1, 2) if other else core)
        at = pl.ds(pl.multiple_of(batch * BATCH, BATCH), BATCH)
        return pltpu.make_async_remote_copy(
            src_ref=chosen_rows.at[at],
            dst_ref=left.at[at, pl.ds(pl.multiple_of(me * columns, columns), columns)],
            send_sem=send_sem.at[batch, index],
            recv_sem=recv_sem.at[batch, y],
            device_id=(following, peer),
            device_id_type=MESH,
        )

    lanes = lax.broadcasted_iota(jnp.int32, (BATCH, rows), 1)

    def advance(batch, _):
        at = pl.ds(pl.multiple_of(batch * BATCH, BATCH), BATCH)
        square = jnp.zeros((BATCH, 128), jnp.float32)
        for count, ahead in enumerate(ORDER):
            chip = lax.rem(y + ahead, chips)
            span = pl.ds(pl.multiple_of(chip * 2 * columns, 2 * columns), 2 * columns)

            @pl.when(jnp.logical_not(first))
            def _():
                pltpu.make_async_copy(left.at[at, span], left.at[at, span], recv_sem.at[batch, chip]).wait()

            x = left[at, span]
            high = x.astype(jnp.bfloat16).astype(jnp.float32)
            both = jnp.concatenate([high, x - high], axis=0).astype(jnp.bfloat16)
            for lane in range(2 * columns // 128):
                piece = x[:, lane * 128 : (lane + 1) * 128]
                square += piece * piece
            product = jnp.dot(both, whi[span, :], preferred_element_type=jnp.float32) + jnp.dot(
                both, wlo[span, :], preferred_element_type=jnp.float32
            )
            product = product[:BATCH] + product[BATCH:]
            if count == 0:
                acc[...] = product
            else:
                acc[...] += product
        norm = jnp.sum(square, axis=1, keepdims=True) / width
        scale = jnp.where(first, 1.0, 1.0 / jnp.sqrt(norm + 1e-06))
        chosen = jnp.zeros((BATCH, columns), jnp.float32)
        weight = jnp.zeros((BATCH, rows), jnp.float32)
        pick = picks[at, 0:1]
        amplitudes = []
        for k in range(outcomes):
            amplitude = acc[:, k * columns : (k + 1) * columns] * scale
            amplitudes.append(amplitude)
            chosen += jnp.where(pick == k, amplitude, 0.0)
        chosen_rows[at, :] = chosen

        @pl.when(jnp.logical_not(last))
        def _():
            for index in range(len(DIRECT)):
                send(batch, index).start()

        for k, amplitude in enumerate(amplitudes):
            squared = jnp.sum(amplitude * amplitude, axis=1, keepdims=True)
            weight += jnp.where(lanes == k, squared, 0.0)
        part[at, :] = weight
        return 0

    lax.fori_loop(0, batches, advance, 0)

    totals[me] = part[...].T[:8]

    def share(ahead):
        return pltpu.make_async_remote_copy(
            src_ref=totals.at[me],
            dst_ref=totals.at[me],
            send_sem=wsend_sem.at[ahead],
            recv_sem=wrecv_sem.at[ahead],
            device_id=(section, lax.rem(me + ahead, peers)),
            device_id_type=MESH,
        )

    for ahead in range(1, peers):
        share(ahead).start()
    for ahead in range(1, peers):
        share(ahead).wait_recv()
    total = totals[0]
    for peer in range(1, peers):
        total += totals[peer]
    whole = jnp.zeros((1, rows), jnp.float32)
    taken = jnp.zeros((1, rows), jnp.float32)
    for k in range(outcomes):
        whole += total[k : k + 1]
        taken += jnp.where(sel_ref[...] == k, total[k : k + 1], 0.0)
    prob_ref[...] = taken / whole
    divisor = jnp.sqrt(taken / width + 1e-06)
    inverse[...] = jnp.broadcast_to(divisor, (rows, rows)).T
    rows_ref[...] = chosen_rows[...] / inverse[:, 0:1]

    for ahead in range(1, peers):
        share(ahead).wait_send()

    @pl.when(jnp.logical_not(last))
    def _():
        def drain(batch, _):
            for index in range(len(DIRECT)):
                send(batch, index).wait_send()
            return 0

        lax.fori_loop(0, batches, drain, 0)


def on_device(site_tensor, boundary, selected):
    _, width, outcomes, columns = site_tensor.shape
    rows = boundary.shape[0]
    peers = lax.axis_size("bond")
    batches = rows // BATCH
    prob, out = pl.pallas_call(
        kernel,
        out_shape=(
            jax.ShapeDtypeStruct((1, rows), jnp.float32),
            jax.ShapeDtypeStruct((rows, columns), jnp.float32),
        ),
        in_specs=[
            pl.BlockSpec(memory_space=pltpu.VMEM),
            pl.BlockSpec(memory_space=pl.ANY),
            pl.BlockSpec(memory_space=pl.ANY),
        ],
        out_specs=(pl.BlockSpec(memory_space=pltpu.VMEM), pl.BlockSpec(memory_space=pltpu.VMEM)),
        scratch_shapes=[
            pltpu.VMEM((SLOTS, FILL, outcomes, columns), jnp.float32),
            pltpu.VMEM((width, outcomes * columns), jnp.bfloat16),
            pltpu.VMEM((width, outcomes * columns), jnp.bfloat16),
            pltpu.VMEM((rows, width), jnp.float32),
            pltpu.VMEM((rows, columns), jnp.float32),
            pltpu.VMEM((BATCH, outcomes * columns), jnp.float32),
            pltpu.VMEM((rows, rows), jnp.float32),
            pltpu.VMEM((rows, rows), jnp.float32),
            pltpu.VMEM((peers, 8, rows), jnp.float32),
            pltpu.VMEM((rows, rows), jnp.float32),
            pltpu.SemaphoreType.DMA((SLOTS,)),
            pltpu.SemaphoreType.DMA,
            pltpu.SemaphoreType.DMA((batches, len(DIRECT))),
            pltpu.SemaphoreType.DMA((batches, peers // 2)),
            pltpu.SemaphoreType.DMA((peers,)),
            pltpu.SemaphoreType.DMA((peers,)),
        ],
        compiler_params=pltpu.CompilerParams(
            collective_id=0, has_side_effects=True, vmem_limit_bytes=60 * 2**20
        ),
    )(selected, site_tensor, boundary)
    return prob, out[None]


def solution(mesh):
    in_specs = (P("section", None, None, "bond"), P(), P("section", None))
    out_specs = (P("section", None), P("section", None, "bond"))
    return jax.shard_map(
        on_device, mesh=mesh, in_specs=in_specs, out_specs=out_specs, check_vma=False
    )
```

```python
import functools

import jax
import jax.numpy as jnp
from jax import lax
from jax.experimental import pallas as pl
from jax.experimental.pallas import tpu as pltpu
from jax.sharding import PartitionSpec as P

MESH = pl.DeviceIdType.MESH
BATCH = 16
FILL = 192
SLOTS = 4
SENDS = (0, 2, 1, 3)
OWN, PASS, OTHER, PAIR = range(4)
STEPS = ((0, OWN), (3, OWN), (0, OTHER), (2, OWN), (1, OWN), (3, OTHER), (2, OTHER), (1, OTHER))


def kernel(
    sel_ref, w_hbm, start_hbm, prob_ref, rows_ref,
    stage, whi, wlo, left, chosen_rows, acc, picks, part, totals, inverse,
    fill_sem, start_sem, send_sem, pass_sem, recv_sem, wsend_sem, wrecv_sem,
):
    rows, width = left.shape
    outcomes, columns = w_hbm.shape[2], w_hbm.shape[3]
    sections, peers = lax.axis_size("section"), lax.axis_size("bond")
    chips = peers // 2
    batches = rows // BATCH
    fills = width // FILL
    section, me = lax.axis_index("section"), lax.axis_index("bond")
    y, core = me // 2, lax.rem(me, 2)
    following = lax.rem(section + 1, sections)
    before = lax.rem(section + sections - 1, sections)
    first, last = section == 0, section == sections - 1

    def fill(step, k):
        slot = lax.rem(step, SLOTS)
        return pltpu.make_async_copy(
            w_hbm.at[0, pl.ds(step * FILL, FILL), k, :], stage.at[slot, k], fill_sem.at[slot, k]
        )

    for step in range(SLOTS):
        for k in range(outcomes):
            fill(step, k).start()

    @pl.when(first)
    def _():
        pltpu.make_async_copy(start_hbm, left, start_sem).start()

    barrier = pltpu.get_barrier_semaphore()
    for peer in range(peers):
        for other in (before, following):
            pl.semaphore_signal(barrier, inc=1, device_id=(other, peer), device_id_type=MESH)
    for ahead in range(1, peers):
        pl.semaphore_signal(
            barrier, inc=1, device_id=(section, lax.rem(me + ahead, peers)), device_id_type=MESH
        )

    picks[...] = jnp.broadcast_to(sel_ref[...].astype(jnp.float32), (rows, rows)).T

    def split(step, _):
        slot = lax.rem(step, SLOTS)
        for k in range(outcomes):
            fill(step, k).wait()

        def some(piece, _):
            row = pl.multiple_of(piece * 32, 32)
            for k in range(outcomes):
                whole = stage[slot, k, pl.ds(row, 32), :]
                high = whole.astype(jnp.bfloat16)
                low = (whole - high.astype(jnp.float32)).astype(jnp.bfloat16)
                at = pl.ds(pl.multiple_of(step * FILL + row, 32), 32)
                whi[at, k * columns : (k + 1) * columns] = high
                wlo[at, k * columns : (k + 1) * columns] = low
            return 0

        lax.fori_loop(0, FILL // 32, some, 0)

        @pl.when(step + SLOTS < fills)
        def _():
            for k in range(outcomes):
                fill(step + SLOTS, k).start()

        return 0

    lax.fori_loop(0, fills, split, 0)

    pl.semaphore_wait(barrier, 3 * peers - 1)

    @pl.when(first)
    def _():
        pltpu.make_async_copy(start_hbm, left, start_sem).wait()

    def rows_of(batch):
        return pl.ds(pl.multiple_of(batch * BATCH, BATCH), BATCH)

    def block_of(source, count=1):
        return pl.ds(pl.multiple_of(source * columns, columns), count * columns)

    def send(batch, index):
        at = rows_of(batch)
        return pltpu.make_async_remote_copy(
            src_ref=chosen_rows.at[at],
            dst_ref=left.at[at, block_of(me)],
            send_sem=send_sem.at[batch, index],
            recv_sem=recv_sem.at[batch, me],
            device_id=(following, lax.rem(y + SENDS[index], chips) * 2 + core),
            device_id_type=MESH,
        )

    def relay(batch, source):
        block = left.at[rows_of(batch), block_of(source)]
        return pltpu.make_async_remote_copy(
            src_ref=block,
            dst_ref=block,
            send_sem=pass_sem.at[batch, source // 2],
            recv_sem=recv_sem.at[batch, source],
            device_id=(section, y * 2 + 1 - core),
            device_id_type=MESH,
        )

    def arrive(batch, source):
        block = left.at[rows_of(batch), block_of(source)]
        pltpu.make_async_copy(block, block, recv_sem.at[batch, source]).wait()

    lanes = lax.broadcasted_iota(jnp.int32, (BATCH, rows), 1)

    def advance(batch, _):
        at = rows_of(batch)
        square = jnp.zeros((BATCH, 128), jnp.float32)
        fresh = True
        for ahead, what in STEPS:
            chip = lax.rem(y + ahead, chips)
            source = chip * 2 + (core if what in (OWN, PASS) else 1 - core)

            @pl.when(jnp.logical_not(first))
            def _():
                arrive(batch, source)
                if what in (OWN, PASS):
                    relay(batch, source).start()

            if what == PASS:
                continue
            span = block_of(chip * 2, 2) if what == PAIR else block_of(source)
            x = left[at, span]
            high = x.astype(jnp.bfloat16).astype(jnp.float32)
            both = jnp.concatenate([high, x - high], axis=0).astype(jnp.bfloat16)
            for lane in range(x.shape[1] // 128):
                piece = x[:, lane * 128 : (lane + 1) * 128]
                square += piece * piece
            product = jnp.dot(both, whi[span, :], preferred_element_type=jnp.float32)
            product = product[:BATCH] + product[BATCH:]
            product += jnp.dot(both[:BATCH], wlo[span, :], preferred_element_type=jnp.float32)
            if fresh:
                acc[...] = product
            else:
                acc[...] += product
            fresh = False
        norm = jnp.sum(square, axis=1, keepdims=True) / width
        scale = jnp.where(first, 1.0, 1.0 / jnp.sqrt(norm + 1e-06))
        chosen = jnp.zeros((BATCH, columns), jnp.float32)
        weight = jnp.zeros((BATCH, rows), jnp.float32)
        pick = picks[at, 0:1]
        amplitudes = []
        for k in range(outcomes):
            amplitude = acc[:, k * columns : (k + 1) * columns] * scale
            amplitudes.append(amplitude)
            chosen += jnp.where(pick == k, amplitude, 0.0)
        chosen_rows[at, :] = chosen

        @pl.when(jnp.logical_not(last))
        def _():
            for index in range(len(SENDS)):
                send(batch, index).start()

        for k, amplitude in enumerate(amplitudes):
            squared = jnp.sum(amplitude * amplitude, axis=1, keepdims=True)
            weight += jnp.where(lanes == k, squared, 0.0)
        part[at, :] = weight
        return 0

    lax.fori_loop(0, batches, advance, 0)

    totals[me] = part[...].T[:8]

    def share(ahead):
        return pltpu.make_async_remote_copy(
            src_ref=totals.at[me],
            dst_ref=totals.at[me],
            send_sem=wsend_sem.at[ahead],
            recv_sem=wrecv_sem.at[ahead],
            device_id=(section, lax.rem(me + ahead, peers)),
            device_id_type=MESH,
        )

    for ahead in range(1, peers):
        share(ahead).start()
    for ahead in range(1, peers):
        share(ahead).wait_recv()
    total = totals[0]
    for peer in range(1, peers):
        total += totals[peer]
    whole = jnp.zeros((1, rows), jnp.float32)
    taken = jnp.zeros((1, rows), jnp.float32)
    for k in range(outcomes):
        whole += total[k : k + 1]
        taken += jnp.where(sel_ref[...] == k, total[k : k + 1], 0.0)
    prob_ref[...] = taken / whole
    divisor = jnp.sqrt(taken / width + 1e-06)
    inverse[...] = jnp.broadcast_to(divisor, (rows, rows)).T
    rows_ref[...] = chosen_rows[...] / inverse[:, 0:1]

    for ahead in range(1, peers):
        share(ahead).wait_send()

    def drain(batch, _):
        @pl.when(jnp.logical_not(last))
        def _():
            for index in range(len(SENDS)):
                send(batch, index).wait_send()

        @pl.when(jnp.logical_not(first))
        def _():
            for chip in range(peers // 2):
                relay(batch, chip * 2 + core).wait_send()

        return 0

    lax.fori_loop(0, batches, drain, 0)


def on_device(site_tensor, boundary, selected):
    _, width, outcomes, columns = site_tensor.shape
    rows = boundary.shape[0]
    peers = lax.axis_size("bond")
    batches = rows // BATCH
    prob, out = pl.pallas_call(
        kernel,
        out_shape=(
            jax.ShapeDtypeStruct((1, rows), jnp.float32),
            jax.ShapeDtypeStruct((rows, columns), jnp.float32),
        ),
        in_specs=[
            pl.BlockSpec(memory_space=pltpu.VMEM),
            pl.BlockSpec(memory_space=pl.ANY),
            pl.BlockSpec(memory_space=pl.ANY),
        ],
        out_specs=(pl.BlockSpec(memory_space=pltpu.VMEM), pl.BlockSpec(memory_space=pltpu.VMEM)),
        scratch_shapes=[
            pltpu.VMEM((SLOTS, outcomes, FILL, columns), jnp.float32),
            pltpu.VMEM((width, outcomes * columns), jnp.bfloat16),
            pltpu.VMEM((width, outcomes * columns), jnp.bfloat16),
            pltpu.VMEM((rows, width), jnp.float32),
            pltpu.VMEM((rows, columns), jnp.float32),
            pltpu.VMEM((BATCH, outcomes * columns), jnp.float32),
            pltpu.VMEM((rows, rows), jnp.float32),
            pltpu.VMEM((rows, rows), jnp.float32),
            pltpu.VMEM((peers, 8, rows), jnp.float32),
            pltpu.VMEM((rows, rows), jnp.float32),
            pltpu.SemaphoreType.DMA((SLOTS, outcomes)),
            pltpu.SemaphoreType.DMA,
            pltpu.SemaphoreType.DMA((batches, len(SENDS))),
            pltpu.SemaphoreType.DMA((batches, peers // 2)),
            pltpu.SemaphoreType.DMA((batches, peers)),
            pltpu.SemaphoreType.DMA((peers,)),
            pltpu.SemaphoreType.DMA((peers,)),
        ],
        compiler_params=pltpu.CompilerParams(
            collective_id=0, has_side_effects=True, vmem_limit_bytes=60 * 2**20
        ),
    )(selected, site_tensor, boundary)
    return prob, out[None]


def solution(mesh):
    in_specs = (P("section", None, None, "bond"), P(), P("section", None))
    out_specs = (P("section", None), P("section", None, "bond"))
    return jax.shard_map(
        on_device, mesh=mesh, in_specs=in_specs, out_specs=out_specs, check_vma=False
    )
```

```python
import functools

import jax
import jax.numpy as jnp
from jax import lax
from jax.experimental import pallas as pl
from jax.experimental.pallas import tpu as pltpu
from jax.sharding import PartitionSpec as P

MESH = pl.DeviceIdType.MESH
BATCH = 16
FILL = 192
SLOTS = 4
SENDS = ((2, 0), (0, 0), (1, 0), (3, 0))
STEPS = ((0, 0), (2, 0), (3, 0), (1, 0), (0, 1), (2, 1), (3, 1), (1, 1))


def kernel(
    sel_ref, w_hbm, start_hbm, prob_ref, rows_ref,
    stage, whi, wlo, left, chosen_rows, acc, picks, part, totals, inverse,
    fill_sem, start_sem, send_sem, pass_sem, recv_sem, wsend_sem, wrecv_sem,
):
    rows, width = left.shape
    outcomes, columns = w_hbm.shape[2], w_hbm.shape[3]
    sections, peers = lax.axis_size("section"), lax.axis_size("bond")
    chips = peers // 2
    batches = rows // BATCH
    fills = width // FILL
    section, me = lax.axis_index("section"), lax.axis_index("bond")
    y, core = me // 2, lax.rem(me, 2)
    following = lax.rem(section + 1, sections)
    before = lax.rem(section + sections - 1, sections)
    first, last = section == 0, section == sections - 1
    passed = [ahead for ahead in range(chips) if ((chips - ahead) % chips, 1) not in SENDS]

    def fill(step, k):
        slot = lax.rem(step, SLOTS)
        return pltpu.make_async_copy(
            w_hbm.at[0, pl.ds(step * FILL, FILL), k, :], stage.at[slot, k], fill_sem.at[slot, k]
        )

    for step in range(SLOTS):
        for k in range(outcomes):
            fill(step, k).start()

    @pl.when(first)
    def _():
        pltpu.make_async_copy(start_hbm, left, start_sem).start()

    barrier = pltpu.get_barrier_semaphore()
    for peer in range(peers):
        for other in (before, following):
            pl.semaphore_signal(barrier, inc=1, device_id=(other, peer), device_id_type=MESH)
    for ahead in range(1, peers):
        pl.semaphore_signal(
            barrier, inc=1, device_id=(section, lax.rem(me + ahead, peers)), device_id_type=MESH
        )

    picks[...] = jnp.broadcast_to(sel_ref[...].astype(jnp.float32), (rows, rows)).T

    def split(step, _):
        slot = lax.rem(step, SLOTS)
        for k in range(outcomes):
            fill(step, k).wait()

        def some(piece, _):
            row = pl.multiple_of(piece * 32, 32)
            for k in range(outcomes):
                whole = stage[slot, k, pl.ds(row, 32), :]
                high = whole.astype(jnp.bfloat16)
                low = (whole - high.astype(jnp.float32)).astype(jnp.bfloat16)
                at = pl.ds(pl.multiple_of(step * FILL + row, 32), 32)
                whi[at, k * columns : (k + 1) * columns] = high
                wlo[at, k * columns : (k + 1) * columns] = low
            return 0

        lax.fori_loop(0, FILL // 32, some, 0)

        @pl.when(step + SLOTS < fills)
        def _():
            for k in range(outcomes):
                fill(step + SLOTS, k).start()

        return 0

    lax.fori_loop(0, fills, split, 0)

    pl.semaphore_wait(barrier, 3 * peers - 1)

    @pl.when(first)
    def _():
        pltpu.make_async_copy(start_hbm, left, start_sem).wait()

    def rows_of(batch):
        return pl.ds(pl.multiple_of(batch * BATCH, BATCH), BATCH)

    def block_of(source, count=1):
        return pl.ds(pl.multiple_of(source * columns, columns), count * columns)

    def send(batch, index):
        at = rows_of(batch)
        ahead, other = SENDS[index]
        return pltpu.make_async_remote_copy(
            src_ref=chosen_rows.at[at],
            dst_ref=left.at[at, block_of(me)],
            send_sem=send_sem.at[batch, index],
            recv_sem=recv_sem.at[batch, me],
            device_id=(following, lax.rem(y + ahead, chips) * 2 + (1 - core if other else core)),
            device_id_type=MESH,
        )

    def relay(batch, source):
        block = left.at[rows_of(batch), block_of(source)]
        return pltpu.make_async_remote_copy(
            src_ref=block,
            dst_ref=block,
            send_sem=pass_sem.at[batch, source // 2],
            recv_sem=recv_sem.at[batch, source],
            device_id=(section, y * 2 + 1 - core),
            device_id_type=MESH,
        )

    def arrive(batch, source):
        block = left.at[rows_of(batch), block_of(source)]
        pltpu.make_async_copy(block, block, recv_sem.at[batch, source]).wait()

    lanes = lax.broadcasted_iota(jnp.int32, (BATCH, rows), 1)

    def advance(fed, batch, _):
        at = rows_of(batch)
        square = jnp.zeros((BATCH, 128), jnp.float32)
        fresh = True
        for ahead, other in STEPS:
            chip = lax.rem(y + ahead, chips)
            source = chip * 2 + (1 - core if other else core)

            if fed:
                arrive(batch, source)
                if not other and ahead in passed:
                    relay(batch, source).start()
            span = block_of(source)
            x = left[at, span]
            high = x.astype(jnp.bfloat16).astype(jnp.float32)
            both = jnp.concatenate([high, x - high], axis=0).astype(jnp.bfloat16)
            for lane in range(x.shape[1] // 128):
                piece = x[:, lane * 128 : (lane + 1) * 128]
                square += piece * piece
            product = jnp.dot(both, whi[span, :], preferred_element_type=jnp.float32)
            product = product[:BATCH] + product[BATCH:]
            product += jnp.dot(both[:BATCH], wlo[span, :], preferred_element_type=jnp.float32)
            if fresh:
                acc[...] = product
            else:
                acc[...] += product
            fresh = False
        norm = jnp.sum(square, axis=1, keepdims=True) / width
        scale = 1.0 / jnp.sqrt(norm + 1e-06) if fed else 1.0
        chosen = jnp.zeros((BATCH, columns), jnp.float32)
        weight = jnp.zeros((BATCH, rows), jnp.float32)
        pick = picks[at, 0:1]
        amplitudes = []
        for k in range(outcomes):
            amplitude = acc[:, k * columns : (k + 1) * columns] * scale
            amplitudes.append(amplitude)
            chosen += jnp.where(pick == k, amplitude, 0.0)
        chosen_rows[at, :] = chosen

        @pl.when(jnp.logical_not(last))
        def _():
            for index in range(len(SENDS)):
                send(batch, index).start()

        for k, amplitude in enumerate(amplitudes):
            squared = jnp.sum(amplitude * amplitude, axis=1, keepdims=True)
            weight += jnp.where(lanes == k, squared, 0.0)
        part[at, :] = weight
        return 0

    @pl.when(first)
    def _():
        lax.fori_loop(0, batches, functools.partial(advance, False), 0)

    @pl.when(jnp.logical_not(first))
    def _():
        lax.fori_loop(0, batches, functools.partial(advance, True), 0)

    totals[me] = part[...].T[:8]

    def share(ahead):
        return pltpu.make_async_remote_copy(
            src_ref=totals.at[me],
            dst_ref=totals.at[me],
            send_sem=wsend_sem.at[ahead],
            recv_sem=wrecv_sem.at[ahead],
            device_id=(section, lax.rem(me + ahead, peers)),
            device_id_type=MESH,
        )

    for ahead in range(1, peers):
        share(ahead).start()
    for ahead in range(1, peers):
        share(ahead).wait_recv()
    total = totals[0]
    for peer in range(1, peers):
        total += totals[peer]
    whole = jnp.zeros((1, rows), jnp.float32)
    taken = jnp.zeros((1, rows), jnp.float32)
    for k in range(outcomes):
        whole += total[k : k + 1]
        taken += jnp.where(sel_ref[...] == k, total[k : k + 1], 0.0)
    prob_ref[...] = taken / whole
    divisor = jnp.sqrt(taken / width + 1e-06)
    inverse[...] = jnp.broadcast_to(divisor, (rows, rows)).T
    rows_ref[...] = chosen_rows[...] / inverse[:, 0:1]

    for ahead in range(1, peers):
        share(ahead).wait_send()

    def drain(batch, _):
        @pl.when(jnp.logical_not(last))
        def _():
            for index in range(len(SENDS)):
                send(batch, index).wait_send()

        @pl.when(jnp.logical_not(first))
        def _():
            for ahead in passed:
                relay(batch, lax.rem(y + ahead, chips) * 2 + core).wait_send()

        return 0

    lax.fori_loop(0, batches, drain, 0)


def on_device(site_tensor, boundary, selected):
    _, width, outcomes, columns = site_tensor.shape
    rows = boundary.shape[0]
    peers = lax.axis_size("bond")
    batches = rows // BATCH
    prob, out = pl.pallas_call(
        kernel,
        out_shape=(
            jax.ShapeDtypeStruct((1, rows), jnp.float32),
            jax.ShapeDtypeStruct((rows, columns), jnp.float32),
        ),
        in_specs=[
            pl.BlockSpec(memory_space=pltpu.VMEM),
            pl.BlockSpec(memory_space=pl.ANY),
            pl.BlockSpec(memory_space=pl.ANY),
        ],
        out_specs=(pl.BlockSpec(memory_space=pltpu.VMEM), pl.BlockSpec(memory_space=pltpu.VMEM)),
        scratch_shapes=[
            pltpu.VMEM((SLOTS, outcomes, FILL, columns), jnp.float32),
            pltpu.VMEM((width, outcomes * columns), jnp.bfloat16),
            pltpu.VMEM((width, outcomes * columns), jnp.bfloat16),
            pltpu.VMEM((rows, width), jnp.float32),
            pltpu.VMEM((rows, columns), jnp.float32),
            pltpu.VMEM((BATCH, outcomes * columns), jnp.float32),
            pltpu.VMEM((rows, rows), jnp.float32),
            pltpu.VMEM((rows, rows), jnp.float32),
            pltpu.VMEM((peers, 8, rows), jnp.float32),
            pltpu.VMEM((rows, rows), jnp.float32),
            pltpu.SemaphoreType.DMA((SLOTS, outcomes)),
            pltpu.SemaphoreType.DMA,
            pltpu.SemaphoreType.DMA((batches, len(SENDS))),
            pltpu.SemaphoreType.DMA((batches, peers // 2)),
            pltpu.SemaphoreType.DMA((batches, peers)),
            pltpu.SemaphoreType.DMA((peers,)),
            pltpu.SemaphoreType.DMA((peers,)),
        ],
        compiler_params=pltpu.CompilerParams(
            collective_id=0, has_side_effects=True, vmem_limit_bytes=60 * 2**20
        ),
    )(selected, site_tensor, boundary)
    return prob, out[None]


def solution(mesh):
    in_specs = (P("section", None, None, "bond"), P(), P("section", None))
    out_specs = (P("section", None), P("section", None, "bond"))
    return jax.shard_map(
        on_device, mesh=mesh, in_specs=in_specs, out_specs=out_specs, check_vma=False
    )
```

```python
import functools

import jax
import jax.numpy as jnp
from jax import lax
from jax.experimental import pallas as pl
from jax.experimental.pallas import tpu as pltpu
from jax.sharding import PartitionSpec as P

MESH = pl.DeviceIdType.MESH
BATCH = 16
SLOTS = 3
SENDS = ((2, 0), (0, 0), (1, 0), (3, 0))
STEPS = ((0, 0), (2, 0), (3, 0), (1, 0), (0, 1), (2, 1), (3, 1), (1, 1))


def kernel(
    sel_ref, w_hbm, start_hbm, sums_ref, raw_ref,
    stage, whi, wlo, left, chosen_rows, acc, picks, part, totals,
    fill_sem, start_sem, send_sem, pass_sem, recv_sem, wsend_sem, wrecv_sem,
):
    rows, width = left.shape
    outcomes, columns = w_hbm.shape[2], w_hbm.shape[3]
    sections, peers = lax.axis_size("section"), lax.axis_size("bond")
    chips = peers // 2
    batches = rows // BATCH
    section, me = lax.axis_index("section"), lax.axis_index("bond")
    y, core = me // 2, lax.rem(me, 2)
    following = lax.rem(section + 1, sections)
    before = lax.rem(section + sections - 1, sections)
    first, last = section == 0, section == sections - 1
    passed = [ahead for ahead in range(chips) if ((chips - ahead) % chips, 1) not in SENDS]

    @pl.when(first)
    def _():
        pltpu.make_async_copy(start_hbm, left, start_sem).start()

    def fill(step, k):
        slot = lax.rem(step, SLOTS)
        return pltpu.make_async_copy(
            w_hbm.at[0, pl.ds(step * columns, columns), k, :], stage.at[slot, k], fill_sem.at[slot, k]
        )

    for step in range(SLOTS):
        for k in range(outcomes):
            fill(step, k).start()

    barrier = pltpu.get_barrier_semaphore()
    for peer in range(peers):
        for other in (before, following):
            pl.semaphore_signal(barrier, inc=1, device_id=(other, peer), device_id_type=MESH)
    for ahead in range(1, peers):
        pl.semaphore_signal(
            barrier, inc=1, device_id=(section, lax.rem(me + ahead, peers)), device_id_type=MESH
        )

    picks[...] = jnp.broadcast_to(sel_ref[...].astype(jnp.float32), (rows, rows)).T

    def rows_of(batch):
        return pl.ds(pl.multiple_of(batch * BATCH, BATCH), BATCH)

    def block_of(source):
        return pl.ds(pl.multiple_of(source * columns, columns), columns)

    def multiply(x, span):
        high = x.astype(jnp.bfloat16).astype(jnp.float32)
        both = jnp.concatenate([high, x - high], axis=0).astype(jnp.bfloat16)
        product = jnp.dot(both, whi[span, :], preferred_element_type=jnp.float32)
        product = product[:BATCH] + product[BATCH:]
        return product + jnp.dot(both[:BATCH], wlo[span, :], preferred_element_type=jnp.float32)

    @pl.when(first)
    def _():
        pltpu.make_async_copy(start_hbm, left, start_sem).wait()
        acc[...] = jnp.zeros_like(acc)

    def split(step, _):
        slot = lax.rem(step, SLOTS)
        for k in range(outcomes):
            fill(step, k).wait()

        def some(piece, _):
            row = pl.multiple_of(piece * 32, 32)
            for k in range(outcomes):
                whole = stage[slot, k, pl.ds(row, 32), :]
                high = whole.astype(jnp.bfloat16)
                low = (whole - high.astype(jnp.float32)).astype(jnp.bfloat16)
                at = pl.ds(pl.multiple_of(step * columns + row, 32), 32)
                whi[at, k * columns : (k + 1) * columns] = high
                wlo[at, k * columns : (k + 1) * columns] = low
            return 0

        lax.fori_loop(0, columns // 32, some, 0)

        @pl.when(step + SLOTS < peers)
        def _():
            for k in range(outcomes):
                fill(step + SLOTS, k).start()

        @pl.when(first)
        def _():
            acc[...] += multiply(left[rows_of(0), block_of(step)], block_of(step))

        return 0

    lax.fori_loop(0, peers, split, 0)

    pl.semaphore_wait(barrier, 3 * peers - 1)

    def send(batch, index):
        at = rows_of(batch)
        ahead, other = SENDS[index]
        return pltpu.make_async_remote_copy(
            src_ref=chosen_rows.at[at],
            dst_ref=left.at[at, block_of(me)],
            send_sem=send_sem.at[batch, index],
            recv_sem=recv_sem.at[batch, me],
            device_id=(following, lax.rem(y + ahead, chips) * 2 + (1 - core if other else core)),
            device_id_type=MESH,
        )

    def relay(batch, source):
        block = left.at[rows_of(batch), block_of(source)]
        return pltpu.make_async_remote_copy(
            src_ref=block,
            dst_ref=block,
            send_sem=pass_sem.at[batch, source // 2],
            recv_sem=recv_sem.at[batch, source],
            device_id=(section, y * 2 + 1 - core),
            device_id_type=MESH,
        )

    def arrive(batch, source):
        block = left.at[rows_of(batch), block_of(source)]
        pltpu.make_async_copy(block, block, recv_sem.at[batch, source]).wait()

    lanes = lax.broadcasted_iota(jnp.int32, (BATCH, rows), 1)

    def advance(fed, done, batch, _):
        at = rows_of(batch)
        square = jnp.zeros((BATCH, 128), jnp.float32)
        fresh = True
        for ahead, other in () if done else STEPS:
            chip = lax.rem(y + ahead, chips)
            source = chip * 2 + (1 - core if other else core)

            if fed:
                arrive(batch, source)
                if not other and ahead in passed:
                    relay(batch, source).start()
            span = block_of(source)
            x = left[at, span]
            for lane in range(columns // 128):
                piece = x[:, lane * 128 : (lane + 1) * 128]
                square += piece * piece
            product = multiply(x, span)
            if fresh:
                acc[...] = product
            else:
                acc[...] += product
            fresh = False
        norm = jnp.sum(square, axis=1, keepdims=True) / width
        scale = 1.0 / jnp.sqrt(norm + 1e-06) if fed else 1.0
        chosen = jnp.zeros((BATCH, columns), jnp.float32)
        weight = jnp.zeros((BATCH, rows), jnp.float32)
        pick = picks[at, 0:1]
        amplitudes = []
        for k in range(outcomes):
            amplitude = acc[:, k * columns : (k + 1) * columns] * scale
            amplitudes.append(amplitude)
            chosen += jnp.where(pick == k, amplitude, 0.0)
        chosen_rows[at, :] = chosen

        @pl.when(jnp.logical_not(last))
        def _():
            for index in range(len(SENDS)):
                send(batch, index).start()

        for k, amplitude in enumerate(amplitudes):
            squared = jnp.sum(amplitude * amplitude, axis=1, keepdims=True)
            weight += jnp.where(lanes == k, squared, 0.0)
        part[at, :] = weight
        return 0

    @pl.when(first)
    def _():
        advance(False, True, 0, 0)
        lax.fori_loop(1, batches, functools.partial(advance, False, False), 0)

    @pl.when(jnp.logical_not(first))
    def _():
        lax.fori_loop(0, batches, functools.partial(advance, True, False), 0)

    result = pltpu.make_async_copy(chosen_rows, raw_ref, start_sem)
    result.start()
    totals[me] = part[...].T[:8]

    def share(ahead):
        return pltpu.make_async_remote_copy(
            src_ref=totals.at[me],
            dst_ref=totals.at[me],
            send_sem=wsend_sem.at[ahead],
            recv_sem=wrecv_sem.at[ahead],
            device_id=(section, lax.rem(me + ahead, peers)),
            device_id_type=MESH,
        )

    for ahead in range(1, peers):
        share(ahead).start()
    for ahead in range(1, peers):
        share(ahead).wait_recv()
    total = totals[0]
    for peer in range(1, peers):
        total += totals[peer]
    whole = jnp.zeros((1, rows), jnp.float32)
    taken = jnp.zeros((1, rows), jnp.float32)
    for k in range(outcomes):
        whole += total[k : k + 1]
        taken += jnp.where(sel_ref[...] == k, total[k : k + 1], 0.0)
    sums_ref[0:1] = taken
    sums_ref[1:2] = whole
    result.wait()

    for ahead in range(1, peers):
        share(ahead).wait_send()

    def drain(batch, _):
        @pl.when(jnp.logical_not(last))
        def _():
            for index in range(len(SENDS)):
                send(batch, index).wait_send()

        @pl.when(jnp.logical_not(first))
        def _():
            for ahead in passed:
                relay(batch, lax.rem(y + ahead, chips) * 2 + core).wait_send()

        return 0

    lax.fori_loop(0, batches, drain, 0)


def finish(width, sums_ref, raw_ref, prob_ref, rows_ref):
    rows = raw_ref.shape[0]
    taken = sums_ref[0:1]
    prob_ref[...] = taken / sums_ref[1:2]
    divisor = jnp.broadcast_to(jnp.sqrt(taken / width + 1e-06), (rows, rows)).T
    rows_ref[0] = raw_ref[...] / divisor[:, 0:1]


def on_device(site_tensor, boundary, selected):
    _, width, outcomes, columns = site_tensor.shape
    rows = boundary.shape[0]
    peers = lax.axis_size("bond")
    batches = rows // BATCH
    sums, raw = pl.pallas_call(
        kernel,
        out_shape=(
            jax.ShapeDtypeStruct((2, rows), jnp.float32),
            jax.ShapeDtypeStruct((rows, columns), jnp.float32),
        ),
        in_specs=[
            pl.BlockSpec(memory_space=pltpu.VMEM),
            pl.BlockSpec(memory_space=pl.ANY),
            pl.BlockSpec(memory_space=pl.ANY),
        ],
        out_specs=(pl.BlockSpec(memory_space=pltpu.VMEM), pl.BlockSpec(memory_space=pl.ANY)),
        scratch_shapes=[
            pltpu.VMEM((SLOTS, outcomes, columns, columns), jnp.float32),
            pltpu.VMEM((width, outcomes * columns), jnp.bfloat16),
            pltpu.VMEM((width, outcomes * columns), jnp.bfloat16),
            pltpu.VMEM((rows, width), jnp.float32),
            pltpu.VMEM((rows, columns), jnp.float32),
            pltpu.VMEM((BATCH, outcomes * columns), jnp.float32),
            pltpu.VMEM((rows, rows), jnp.float32),
            pltpu.VMEM((rows, rows), jnp.float32),
            pltpu.VMEM((peers, 8, rows), jnp.float32),
            pltpu.SemaphoreType.DMA((SLOTS, outcomes)),
            pltpu.SemaphoreType.DMA,
            pltpu.SemaphoreType.DMA((batches, len(SENDS))),
            pltpu.SemaphoreType.DMA((batches, peers // 2)),
            pltpu.SemaphoreType.DMA((batches, peers)),
            pltpu.SemaphoreType.DMA((peers,)),
            pltpu.SemaphoreType.DMA((peers,)),
        ],
        compiler_params=pltpu.CompilerParams(
            collective_id=0, has_side_effects=True, vmem_limit_bytes=60 * 2**20
        ),
    )(selected, site_tensor, boundary)
    return pl.pallas_call(
        functools.partial(finish, width),
        out_shape=(
            jax.ShapeDtypeStruct((1, rows), jnp.float32),
            jax.ShapeDtypeStruct((1, rows, columns), jnp.float32),
        ),
        in_specs=[pl.BlockSpec(memory_space=pltpu.VMEM)] * 2,
        out_specs=(pl.BlockSpec(memory_space=pltpu.VMEM), pl.BlockSpec(memory_space=pltpu.VMEM)),
    )(sums, raw)


def solution(mesh):
    in_specs = (P("section", None, None, "bond"), P(), P("section", None))
    out_specs = (P("section", None), P("section", None, "bond"))
    return jax.shard_map(
        on_device, mesh=mesh, in_specs=in_specs, out_specs=out_specs, check_vma=False
    )
```

```python
import functools

import jax
import jax.numpy as jnp
from jax import lax
from jax.experimental import pallas as pl
from jax.experimental.pallas import tpu as pltpu
from jax.sharding import PartitionSpec as P

MESH = pl.DeviceIdType.MESH
BATCH = 16
SLOTS = 3
SENDS = ((2, 0), (0, 0), (1, 0), (3, 0))
STEPS = ((0, 0), (2, 0), (3, 0), (1, 0), (0, 1), (2, 1), (3, 1), (1, 1))


def kernel(
    sel_ref, w_hbm, start_hbm, sums_ref, raw_ref,
    stage, whi, wlo, left, chosen_rows, acc, picks, part, totals,
    fill_sem, start_sem, send_sem, pass_sem, recv_sem, wsend_sem, wrecv_sem,
):
    rows, width = left.shape
    outcomes, columns = w_hbm.shape[2], w_hbm.shape[3]
    sections, peers = lax.axis_size("section"), lax.axis_size("bond")
    chips = peers // 2
    batches = rows // BATCH
    section, me = lax.axis_index("section"), lax.axis_index("bond")
    y, core = me // 2, lax.rem(me, 2)
    following = lax.rem(section + 1, sections)
    before = lax.rem(section + sections - 1, sections)
    first, last = section == 0, section == sections - 1
    passed = [ahead for ahead in range(chips) if ((chips - ahead) % chips, 1) not in SENDS]

    @pl.when(first)
    def _():
        pltpu.make_async_copy(start_hbm, left, start_sem).start()

    def fill(step, k):
        slot = lax.rem(step, SLOTS)
        return pltpu.make_async_copy(
            w_hbm.at[0, pl.ds(step * columns, columns), k, :], stage.at[slot, k], fill_sem.at[slot, k]
        )

    for step in range(SLOTS):
        for k in range(outcomes):
            fill(step, k).start()

    barrier = pltpu.get_barrier_semaphore()
    for peer in range(peers):
        for other in (before, following):
            pl.semaphore_signal(barrier, inc=1, device_id=(other, peer), device_id_type=MESH)
    for ahead in range(1, peers):
        pl.semaphore_signal(
            barrier, inc=1, device_id=(section, lax.rem(me + ahead, peers)), device_id_type=MESH
        )

    picks[...] = jnp.broadcast_to(sel_ref[...].astype(jnp.float32), (rows, rows)).T

    def along(ahead, owner):
        return lax.rem(y + ahead + owner * (2 * chips - 2 * ahead), chips)

    def rows_of(batch):
        return pl.ds(pl.multiple_of(batch * BATCH, BATCH), BATCH)

    def block_of(source):
        return pl.ds(pl.multiple_of(source * columns, columns), columns)

    def multiply(x, span):
        high = x.astype(jnp.bfloat16).astype(jnp.float32)
        both = jnp.concatenate([high, x - high], axis=0).astype(jnp.bfloat16)
        product = jnp.dot(both, whi[span, :], preferred_element_type=jnp.float32)
        product = product[:BATCH] + product[BATCH:]
        return product + jnp.dot(both[:BATCH], wlo[span, :], preferred_element_type=jnp.float32)

    @pl.when(first)
    def _():
        pltpu.make_async_copy(start_hbm, left, start_sem).wait()
        acc[...] = jnp.zeros_like(acc)

    def split(step, _):
        slot = lax.rem(step, SLOTS)
        for k in range(outcomes):
            fill(step, k).wait()

        def some(piece, _):
            row = pl.multiple_of(piece * 32, 32)
            for k in range(outcomes):
                whole = stage[slot, k, pl.ds(row, 32), :]
                high = whole.astype(jnp.bfloat16)
                low = (whole - high.astype(jnp.float32)).astype(jnp.bfloat16)
                at = pl.ds(pl.multiple_of(step * columns + row, 32), 32)
                whi[at, k * columns : (k + 1) * columns] = high
                wlo[at, k * columns : (k + 1) * columns] = low
            return 0

        lax.fori_loop(0, columns // 32, some, 0)

        @pl.when(step + SLOTS < peers)
        def _():
            for k in range(outcomes):
                fill(step + SLOTS, k).start()

        @pl.when(first)
        def _():
            acc[...] += multiply(left[rows_of(0), block_of(step)], block_of(step))

        return 0

    lax.fori_loop(0, peers, split, 0)

    pl.semaphore_wait(barrier, 3 * peers - 1)

    def send(batch, index):
        at = rows_of(batch)
        ahead, other = SENDS[index]
        return pltpu.make_async_remote_copy(
            src_ref=chosen_rows.at[at],
            dst_ref=left.at[at, block_of(me)],
            send_sem=send_sem.at[batch, index],
            recv_sem=recv_sem.at[batch, me],
            device_id=(following, along(ahead, core) * 2 + (1 - core if other else core)),
            device_id_type=MESH,
        )

    def relay(batch, source):
        block = left.at[rows_of(batch), block_of(source)]
        return pltpu.make_async_remote_copy(
            src_ref=block,
            dst_ref=block,
            send_sem=pass_sem.at[batch, source // 2],
            recv_sem=recv_sem.at[batch, source],
            device_id=(section, y * 2 + 1 - core),
            device_id_type=MESH,
        )

    def arrive(batch, source):
        block = left.at[rows_of(batch), block_of(source)]
        pltpu.make_async_copy(block, block, recv_sem.at[batch, source]).wait()

    lanes = lax.broadcasted_iota(jnp.int32, (BATCH, rows), 1)

    def advance(fed, done, batch, _):
        at = rows_of(batch)
        square = jnp.zeros((BATCH, 128), jnp.float32)
        fresh = True
        for ahead, other in () if done else STEPS:
            owner = 1 - core if other else core
            source = along(ahead, owner) * 2 + owner

            if fed:
                arrive(batch, source)
                if not other and ahead in passed:
                    relay(batch, source).start()
            span = block_of(source)
            x = left[at, span]
            for lane in range(columns // 128):
                piece = x[:, lane * 128 : (lane + 1) * 128]
                square += piece * piece
            product = multiply(x, span)
            if fresh:
                acc[...] = product
            else:
                acc[...] += product
            fresh = False
        norm = jnp.sum(square, axis=1, keepdims=True) / width
        scale = 1.0 / jnp.sqrt(norm + 1e-06) if fed else 1.0
        chosen = jnp.zeros((BATCH, columns), jnp.float32)
        weight = jnp.zeros((BATCH, rows), jnp.float32)
        pick = picks[at, 0:1]
        amplitudes = []
        for k in range(outcomes):
            amplitude = acc[:, k * columns : (k + 1) * columns] * scale
            amplitudes.append(amplitude)
            chosen += jnp.where(pick == k, amplitude, 0.0)
        chosen_rows[at, :] = chosen

        @pl.when(jnp.logical_not(last))
        def _():
            for index in range(len(SENDS)):
                send(batch, index).start()

        for k, amplitude in enumerate(amplitudes):
            squared = jnp.sum(amplitude * amplitude, axis=1, keepdims=True)
            weight += jnp.where(lanes == k, squared, 0.0)
        part[at, :] = weight
        return 0

    @pl.when(first)
    def _():
        advance(False, True, 0, 0)
        lax.fori_loop(1, batches, functools.partial(advance, False, False), 0)

    @pl.when(jnp.logical_not(first))
    def _():
        lax.fori_loop(0, batches, functools.partial(advance, True, False), 0)

    result = pltpu.make_async_copy(chosen_rows, raw_ref, start_sem)
    result.start()
    totals[me] = part[...].T[:8]

    def share(ahead):
        return pltpu.make_async_remote_copy(
            src_ref=totals.at[me],
            dst_ref=totals.at[me],
            send_sem=wsend_sem.at[ahead],
            recv_sem=wrecv_sem.at[ahead],
            device_id=(section, lax.rem(me + ahead, peers)),
            device_id_type=MESH,
        )

    for ahead in range(1, peers):
        share(ahead).start()
    for ahead in range(1, peers):
        share(ahead).wait_recv()
    total = totals[0]
    for peer in range(1, peers):
        total += totals[peer]
    whole = jnp.zeros((1, rows), jnp.float32)
    taken = jnp.zeros((1, rows), jnp.float32)
    for k in range(outcomes):
        whole += total[k : k + 1]
        taken += jnp.where(sel_ref[...] == k, total[k : k + 1], 0.0)
    sums_ref[0:1] = taken
    sums_ref[1:2] = whole
    result.wait()

    for ahead in range(1, peers):
        share(ahead).wait_send()

    def drain(batch, _):
        @pl.when(jnp.logical_not(last))
        def _():
            for index in range(len(SENDS)):
                send(batch, index).wait_send()

        @pl.when(jnp.logical_not(first))
        def _():
            for ahead in passed:
                relay(batch, lax.rem(y + ahead, chips) * 2 + core).wait_send()

        return 0

    lax.fori_loop(0, batches, drain, 0)


def finish(width, sums_ref, raw_ref, prob_ref, rows_ref):
    rows = raw_ref.shape[0]
    taken = sums_ref[0:1]
    prob_ref[...] = taken / sums_ref[1:2]
    divisor = jnp.broadcast_to(jnp.sqrt(taken / width + 1e-06), (rows, rows)).T
    rows_ref[0] = raw_ref[...] / divisor[:, 0:1]


def on_device(site_tensor, boundary, selected):
    _, width, outcomes, columns = site_tensor.shape
    rows = boundary.shape[0]
    peers = lax.axis_size("bond")
    batches = rows // BATCH
    sums, raw = pl.pallas_call(
        kernel,
        out_shape=(
            jax.ShapeDtypeStruct((2, rows), jnp.float32),
            jax.ShapeDtypeStruct((rows, columns), jnp.float32),
        ),
        in_specs=[
            pl.BlockSpec(memory_space=pltpu.VMEM),
            pl.BlockSpec(memory_space=pl.ANY),
            pl.BlockSpec(memory_space=pl.ANY),
        ],
        out_specs=(pl.BlockSpec(memory_space=pltpu.VMEM), pl.BlockSpec(memory_space=pl.ANY)),
        scratch_shapes=[
            pltpu.VMEM((SLOTS, outcomes, columns, columns), jnp.float32),
            pltpu.VMEM((width, outcomes * columns), jnp.bfloat16),
            pltpu.VMEM((width, outcomes * columns), jnp.bfloat16),
            pltpu.VMEM((rows, width), jnp.float32),
            pltpu.VMEM((rows, columns), jnp.float32),
            pltpu.VMEM((BATCH, outcomes * columns), jnp.float32),
            pltpu.VMEM((rows, rows), jnp.float32),
            pltpu.VMEM((rows, rows), jnp.float32),
            pltpu.VMEM((peers, 8, rows), jnp.float32),
            pltpu.SemaphoreType.DMA((SLOTS, outcomes)),
            pltpu.SemaphoreType.DMA,
            pltpu.SemaphoreType.DMA((batches, len(SENDS))),
            pltpu.SemaphoreType.DMA((batches, peers // 2)),
            pltpu.SemaphoreType.DMA((batches, peers)),
            pltpu.SemaphoreType.DMA((peers,)),
            pltpu.SemaphoreType.DMA((peers,)),
        ],
        compiler_params=pltpu.CompilerParams(
            collective_id=0, has_side_effects=True, vmem_limit_bytes=60 * 2**20
        ),
    )(selected, site_tensor, boundary)
    return pl.pallas_call(
        functools.partial(finish, width),
        out_shape=(
            jax.ShapeDtypeStruct((1, rows), jnp.float32),
            jax.ShapeDtypeStruct((1, rows, columns), jnp.float32),
        ),
        in_specs=[pl.BlockSpec(memory_space=pltpu.VMEM)] * 2,
        out_specs=(pl.BlockSpec(memory_space=pltpu.VMEM), pl.BlockSpec(memory_space=pltpu.VMEM)),
    )(sums, raw)


def solution(mesh):
    in_specs = (P("section", None, None, "bond"), P(), P("section", None))
    out_specs = (P("section", None), P("section", None, "bond"))
    return jax.shard_map(
        on_device, mesh=mesh, in_specs=in_specs, out_specs=out_specs, check_vma=False
    )
```
